512 devices in a mesh: ra: 64 (over x_lo, z, core), band: 8 (over x_hi, y).
Axes of the slice: x: 4 (x_hi: 2, x_lo: 2; x = x_hi * 2 + x_lo), y: 4, z: 16, core: 2. Of those that a mesh axis runs over, the one named last changes fastest.
Arguments:
- tiles: bfloat16 [16384, 64, 128], P(('ra', 'band')), may hold values from -6 to 6
- tile_patch: int32 [16384], P(('ra', 'band')), may hold values from 0 to 63, as said below
- tile_offset: int32 [16384], P(('ra', 'band')), may hold values from 0 to 128
- tile_weight: bfloat16 [16384], P(('ra', 'band')), may hold values from 0.25 to 4
- visit_band: int32 [2048], P(('ra', 'band')), may hold values from 0 to 5
- coeff_index: int32 [16384], P(('ra', 'band')), may hold values from 0 to 63
- coeff_table: float32 [64, 21], replicated, may hold values from -1.3 to 1.3
- row_kernels: bfloat16 [21, 21], replicated, may hold values from -1.25 to 1.25
- column_kernels: bfloat16 [21, 21], replicated, may hold values from -1.25 to 1.25
- band_weight: float32 [6], replicated, may hold values from 0.3 to 1.5
Outputs:
- band_coadds: float32 [6, 64, 16384], P(None, 'band', 'ra')
- detection: float32 [64, 16384], P('band', 'ra')
The draws below stay inside these ranges and needn't reach their ends.
Inputs may be any that keep to these rules, and one draw needn't show every extreme that they name: `tile_patch`: tile j is owned by RA index o = j // 256 and by group g = (j // 32) % 8 of visit owners; its patch lies within 2 patches of o around the cycle of 64 patches. Among the tiles of one device at most 16 fall on one patch, and in every draw, for each group g, one patch receives exactly 16 tiles from each of the 5 devices of group g within reach.
All inputs are finite; a program needn't handle non-finite values.
Results may differ from the reference program's by a relative error of at most 0.005.
Values may be sent and summed in bfloat16 or wider, within the bound.
A program may use at most 64 MiB of HBM per device.

```python
import math
import jax
import jax.numpy as jnp
from jax import lax

ROWS = 64
TW = 128
PW = 256
TAPS = 21
BASIS = 21
BANDS = 6
NTAB = 64
REACH = 2
TILES_VISIT = 8
TILES_DEV = 32
CAP = 16
PATCHES = 64
GROUPS = 8
TILES = 16384
VISITS = 2048


def draw_tile_patch(key, part):
    base = jax.random.fold_in(key, 7)
    key_hot, key_heavy, key_other, key_order = jax.random.split(base, 4)
    hot_patch = jax.random.randint(key_hot, (GROUPS,), 0, PATCHES)
    owner_ra = jnp.arange(PATCHES, dtype=jnp.int32)[:, None]
    distance = (hot_patch[None, :] - owner_ra + PATCHES // 2) % PATCHES - PATCHES // 2
    random_heavy = jax.random.randint(key_heavy, (PATCHES, GROUPS), -REACH, REACH + 1)
    heavy = jnp.where(jnp.abs(distance) <= REACH, distance, random_heavy)
    candidate = jax.random.randint(key_other, (PATCHES, GROUPS, TILES_DEV), 0, 2 * REACH) - REACH
    other = jnp.where(candidate >= heavy[:, :, None], candidate + 1, candidate)
    scores = jax.random.randint(key_order, (PATCHES, GROUPS, TILES_DEV), 0, 1 << 20) * TILES_DEV + jnp.arange(TILES_DEV, dtype=jnp.int32)
    order_rank = jnp.argsort(jnp.argsort(scores, axis=-1), axis=-1)
    offsets = jnp.where(order_rank < CAP, heavy[:, :, None], other)
    return ((owner_ra[:, :, None] + offsets) % PATCHES).reshape(-1).astype(jnp.int32)


def touch_ends(entries, stream_key, least, high):
    dims = entries.shape
    spot = [jax.random.randint(jax.random.fold_in(stream_key, axis), (), 0, dims[axis]) for axis in range(len(dims))]
    entries = entries.at[tuple(spot)].set(least)
    longest = dims.index(max(dims))
    spot[longest] = (spot[longest] + 1) % dims[longest]
    return entries.at[tuple(spot)].set(high)


def levels(key, shape, cuts, least, top_value):
    level, own = 1.0, jax.random.fold_in(key, 6)
    for dim, blocks in cuts:
        steps = jnp.exp(jax.random.uniform(jax.random.fold_in(own, dim), (blocks,), jnp.float32, least / len(cuts), top_value / len(cuts)))
        level = level * jnp.repeat(steps, shape[dim] // blocks).reshape([-1 if axis == dim else 1 for axis in range(len(shape))])
    return level


def scatter_about(rng, dims, width, bound, pieces=(), held_as=jnp.bfloat16):
    factor_of = levels(rng, dims, pieces, -0.22, 0.18) if pieces else 1.0
    entries = jax.random.normal(rng, dims, jnp.float32) * width * factor_of
    return jnp.minimum(jnp.maximum(entries, -bound), bound).astype(held_as)


def setup_inputs(seed: int = 0) -> dict:
    splits = jax.random.split(jax.random.key(seed), 11)
    return {
        "tiles": scatter_about(splits[0], (TILES, ROWS, TW), 1.0, 6.0, ((0, 512),)),
        "tile_patch": draw_tile_patch(jax.random.fold_in(splits[10], 71), 0),
        "tile_offset": touch_ends(jax.random.randint(splits[2], (TILES,), 0, PW - TW + 1), jax.random.fold_in(splits[2], 1), 0, PW - TW).astype(jnp.int32),
        "tile_weight": jnp.clip(jnp.exp(math.log(4.0) - 2.7725887 * jax.random.uniform(splits[3], (TILES,), jnp.float32) ** levels(splits[3], (TILES,), ((0, 512),), -0.2, 0.2)), 0.25, 4.0).astype(jnp.bfloat16),
        "visit_band": touch_ends(jax.random.randint(splits[4], (VISITS,), 0, BANDS), jax.random.fold_in(splits[4], 1), 0, BANDS - 1).astype(jnp.int32),
        "coeff_index": touch_ends(jax.random.randint(splits[5], (TILES,), 0, NTAB), jax.random.fold_in(splits[5], 1), 0, NTAB - 1).astype(jnp.int32),
        "coeff_table": scatter_about(splits[6], (NTAB, BASIS), 0.22, 1.3, (), jnp.float32),
        "row_kernels": scatter_about(splits[7], (BASIS, TAPS), TAPS ** -0.5, 1.25),
        "column_kernels": scatter_about(splits[8], (BASIS, TAPS), TAPS ** -0.5, 1.25),
        "band_weight": jnp.clip(jnp.exp(jax.random.uniform(splits[9], (BANDS,), jnp.float32, math.log(0.3), math.log(1.5))), 0.3, 1.5),
    }


HIGHEST_PRECISION = lax.Precision.HIGHEST


def band_matrices(kernels, extent):
    tap_count = kernels.shape[1]
    tap_of = jnp.arange(extent)[None, :] - jnp.arange(extent)[:, None] + tap_count // 2
    tap_hits = (tap_of[None, :, :] == jnp.arange(tap_count)[:, None, None]).astype(jnp.float32)
    return jnp.einsum("kl,lab->kab", kernels.astype(jnp.float32), tap_hits, precision=HIGHEST_PRECISION)


def reference(tiles, tile_patch, tile_offset, tile_weight, visit_band, coeff_index, coeff_table, row_kernels, column_kernels, band_weight):
    rowmats = band_matrices(row_kernels, ROWS)
    colmats = band_matrices(column_kernels, TW)
    tile_band = jnp.repeat(visit_band, TILES_VISIT).astype(jnp.int32)
    coeffs = jnp.take(coeff_table, coeff_index, axis=0)
    group_size = 16
    groups_total = TILES // group_size
    blocks = (tiles.reshape(groups_total, group_size, ROWS, TW),
              coeffs.reshape(groups_total, group_size, BASIS),
              tile_patch.astype(jnp.int32).reshape(groups_total, group_size),
              tile_offset.astype(jnp.int32).reshape(groups_total, group_size),
              tile_weight.reshape(groups_total, group_size),
              tile_band.reshape(groups_total, group_size))
    zero_index = jnp.zeros((), jnp.int32)

    def one_block(carry, block_in):
        tiles_in, coeff_in, patch_in, offset_in, weight_in, band_in = block_in
        column_pass = jnp.einsum("jic,kdc->jkid", tiles_in.astype(jnp.float32), colmats, precision=HIGHEST_PRECISION).astype(jnp.bfloat16)
        scaled = (coeff_in[:, :, None, None] * rowmats[None]).astype(jnp.bfloat16)
        matched = jnp.einsum("jkab,jkbd->jad", scaled.astype(jnp.float32), column_pass.astype(jnp.float32), precision=HIGHEST_PRECISION).astype(jnp.bfloat16)

        def add_one(position, state):
            numerator, weight_sum = state
            patch_at = patch_in[position]
            band_at = band_in[position]
            offset_at = offset_in[position]
            weight_at = weight_in[position].astype(jnp.float32)
            current = lax.dynamic_slice(numerator, (patch_at, band_at, zero_index, offset_at), (1, 1, ROWS, TW))
            numerator = lax.dynamic_update_slice(numerator, current + weight_at * matched[position].astype(jnp.float32)[None, None], (patch_at, band_at, zero_index, offset_at))
            current_weight = lax.dynamic_slice(weight_sum, (patch_at, band_at, offset_at), (1, 1, TW))
            weight_sum = lax.dynamic_update_slice(weight_sum, current_weight + weight_at, (patch_at, band_at, offset_at))
            return numerator, weight_sum

        return lax.fori_loop(0, group_size, add_one, carry), None

    start_state = (jnp.zeros((PATCHES, BANDS, ROWS, PW), jnp.float32), jnp.zeros((PATCHES, BANDS, PW), jnp.float32))
    (numerator, weight_sum), unused = lax.scan(one_block, start_state, blocks)
    coadds = numerator / jnp.maximum(weight_sum, 1.0)[:, :, None, :]
    band_coadds = jnp.transpose(coadds, (1, 2, 0, 3)).reshape(BANDS, ROWS, PATCHES * PW)
    detection = jnp.einsum("b,brq->rq", band_weight, band_coadds, precision=HIGHEST_PRECISION)
    return band_coadds, detection
```

```python
import jax
import jax.numpy as jnp
from jax import lax
from jax.experimental import pallas as pl
from jax.experimental.pallas import tpu as pltpu
from jax.sharding import PartitionSpec as P

PW = 256
BANDS = 6
REACH = 2
SPREAD = 2 * REACH + 1
F32 = jnp.float32
BF16 = jnp.bfloat16
MESH = pl.DeviceIdType.MESH
SIDES = [p for p in range(SPREAD) if p != REACH]


def kernel(
    n_ra,
    n_band,
    patch_s,
    off_s,
    vband_s,
    cidx_s,
    bw_s,
    ctab_s,
    tiles,
    wt,
    rowk,
    colk,
    out_ref,
    det_ref,
    kpad,
    rbase,
    cst,
    ps,
    mat,
    placed,
    a8,
    nbuf,
    own,
    recva,
    sumb,
    recvb,
    wbuf,
    wrecva,
    wsum,
    wrecvb,
    send_a,
    recv_a,
    send_b,
    recv_b,
    wsend_a,
    wrecv_a,
    wsend_b,
    wrecv_b,
):
    me_ra = lax.axis_index("ra")
    me_band = lax.axis_index("band")
    count, rows, width = tiles.shape
    basis, taps = rowk.shape
    half = taps // 2
    block = rows // n_band
    per_visit = count // vband_s.shape[0]

    def ra_at(distance):
        return lax.rem(me_ra + distance + n_ra, n_ra)

    def band_at(distance):
        return lax.rem(me_band + distance, n_band)

    barrier = pltpu.get_barrier_semaphore()
    for p in SIDES:
        pl.semaphore_signal(
            barrier, inc=1, device_id=(ra_at(p - REACH), me_band), device_id_type=MESH
        )
    for d in range(1, n_band):
        pl.semaphore_signal(
            barrier, inc=1, device_id=(me_ra, band_at(d)), device_id_type=MESH
        )

    lane = lax.broadcasted_iota(jnp.int32, (block, width), 1)
    sub = lax.broadcasted_iota(jnp.int32, (block, width), 0)
    kpad[...] = jnp.zeros_like(kpad)
    kpad[0:basis, 0:taps] = rowk[...].astype(F32)
    for k in range(basis):
        row = jnp.broadcast_to(kpad[k : k + 1, :], (block, width))
        rbase[k * block : (k + 1) * block, :] = pltpu.roll(
            row, width - half, 1, stride=1, stride_axis=0
        )
    kpad[0:basis, 0:taps] = colk[...].astype(F32)
    flip_r = lax.broadcasted_iota(jnp.int32, (width, width), 0)
    flip_c = lax.broadcasted_iota(jnp.int32, (width, width), 1)
    flip = jnp.where(flip_r + flip_c == taps - 1, 1.0, 0.0).astype(BF16)
    kpad[...] = jnp.dot(kpad[...].astype(BF16), flip, preferred_element_type=F32)

    def column_matrix(k, carry):
        row = jnp.broadcast_to(kpad[pl.ds(k, 1), :], (block, width))
        base = pltpu.roll(row, width - half, 1, stride=1, stride_axis=0)
        for c in range(0, width, 2 * block):
            parts = []
            for at in (c, c + block):
                part = base if at == 0 else pltpu.roll(base, at, 1)
                if at < half or at + block > width - half:
                    part = jnp.where(jnp.abs(lane - sub - at) <= half, part, 0.0)
                parts.append(part)
            cst[pl.ds(k * width + c, 2 * block), :] = jnp.concatenate(parts, axis=0).astype(BF16)
        return carry

    lax.fori_loop(0, basis, column_matrix, 0)

    spread_r = lax.broadcasted_iota(jnp.int32, (count, count * block), 0)
    spread_c = lax.broadcasted_iota(jnp.int32, (count, count * block), 1)
    spread = jnp.where(spread_c // block == spread_r, 1.0, 0.0).astype(BF16)
    w_lane = jnp.dot(
        jnp.broadcast_to(wt[...], (block, count)), spread, preferred_element_type=F32
    )
    lane8 = lax.broadcasted_iota(jnp.int32, (block, count * block), 1)
    sub8 = lax.broadcasted_iota(jnp.int32, (block, count * block), 0)
    bucket = jnp.zeros((block, count * block), jnp.int32)
    band = jnp.zeros((block, count * block), jnp.int32)
    for j in range(count):
        here = lane8 // block == j
        bucket = jnp.where(here, patch_s[j], bucket)
        band = jnp.where(here, vband_s[j // per_visit], band)
    bucket = bucket - me_ra + REACH
    bucket = jnp.where(bucket < 0, bucket + n_ra, bucket)
    bucket = jnp.where(bucket >= n_ra, bucket - n_ra, bucket)
    diag = lax.rem(lane8, block) == sub8
    for p in range(SPREAD):
        for b in range(0, BANDS, 2):
            parts = [
                jnp.where((bucket == p) & (band == b + h) & diag, w_lane, 0.0) for h in (0, 1)
            ]
            at = (p * BANDS + b) * block
            a8[at : at + 2 * block, :] = jnp.concatenate(parts, axis=0).astype(BF16)
    first = lax.rem(lane8, block) == 0
    aw = jnp.concatenate(
        [
            jnp.where((bucket == p) & (band == sub8) & first, w_lane, 0.0)
            for p in range(SPREAD)
        ]
        + [jnp.zeros((block, count * block), F32)],
        axis=0,
    ).astype(BF16)

    def cover(jp, carry):
        left, right = [], []
        for h in (0, 1):
            off = off_s[2 * jp + h]
            left.append(jnp.where(lane >= off, 1.0, 0.0))
            right.append(jnp.where(lane < off, 1.0, 0.0))
        at = pl.ds(pl.multiple_of(jp * 2 * block, 2 * block), 2 * block)
        placed[at, 0:width] = jnp.concatenate(left, axis=0).astype(BF16)
        placed[at, width : 2 * width] = jnp.concatenate(right, axis=0).astype(BF16)
        return carry

    lax.fori_loop(0, count // 2, cover, 0)
    sums = jnp.dot(aw, placed[...], preferred_element_type=F32)
    for p in range(SPREAD):
        wbuf[p] = sums[p * block : (p + 1) * block]

    def weight_a(i):
        p = SIDES[i]
        return pltpu.make_async_remote_copy(
            src_ref=wbuf.at[p],
            dst_ref=wrecva.at[i],
            send_sem=wsend_a.at[i],
            recv_sem=wrecv_a.at[i],
            device_id=(ra_at(p - REACH), me_band),
            device_id_type=MESH,
        )

    def weight_b(d):
        return pltpu.make_async_remote_copy(
            src_ref=wsum,
            dst_ref=wrecvb.at[d - 1],
            send_sem=wsend_b.at[d - 1],
            recv_sem=wrecv_b.at[d - 1],
            device_id=(me_ra, band_at(d)),
            device_id_type=MESH,
        )

    def part_a(i, s):
        p = SIDES[i]
        return pltpu.make_async_remote_copy(
            src_ref=nbuf.at[s, i],
            dst_ref=recva.at[s, i],
            send_sem=send_a.at[s, i],
            recv_sem=recv_a.at[s, i],
            device_id=(ra_at(p - REACH), me_band),
            device_id_type=MESH,
        )

    def part_b(s):
        return pltpu.make_async_remote_copy(
            src_ref=sumb.at[s],
            dst_ref=recvb.at[s],
            send_sem=send_b.at[s],
            recv_sem=recv_b.at[s],
            device_id=(me_ra, band_at(s + 1)),
            device_id_type=MESH,
        )

    def compute(s):
        r = lax.rem(me_band + 1 + s, n_band)
        taps_now = pltpu.roll(rbase[...], r * block, 1)[:, 0:rows].astype(BF16)

        def pair(jp, carry):
            t = jnp.concatenate([tiles[2 * jp], tiles[2 * jp + 1]], axis=1)
            x = jnp.dot(taps_now, t, preferred_element_type=F32)
            i0 = cidx_s[2 * jp]
            i1 = cidx_s[2 * jp + 1]
            at = pl.ds(pl.multiple_of(jp * 2 * block, 2 * block), 2 * block)
            for k in range(basis):
                x0 = x[k * block : (k + 1) * block, 0:width] * ctab_s[i0, k]
                x1 = x[k * block : (k + 1) * block, width : 2 * width] * ctab_s[i1, k]
                ps[at, k * width : (k + 1) * width] = jnp.concatenate([x0, x1], axis=0).astype(BF16)
            return carry

        lax.fori_loop(0, count // 2, pair, 0)
        mat[...] = jnp.dot(ps[...], cst[...], preferred_element_type=F32)

        def place(jp, carry):
            left, right = [], []
            for h in (0, 1):
                off = off_s[2 * jp + h]
                at = pl.ds(pl.multiple_of((2 * jp + h) * block, block), block)
                moved = pltpu.roll(mat[at, :], off, 1)
                left.append(jnp.where(lane >= off, moved, 0.0))
                right.append(jnp.where(lane < off, moved, 0.0))
            at = pl.ds(pl.multiple_of(jp * 2 * block, 2 * block), 2 * block)
            placed[at, 0:width] = jnp.concatenate(left, axis=0).astype(BF16)
            placed[at, width : 2 * width] = jnp.concatenate(right, axis=0).astype(BF16)
            return carry

        lax.fori_loop(0, count // 2, place, 0)
        n = jnp.dot(a8[...], placed[...], preferred_element_type=F32)
        size = BANDS * block
        for i, p in enumerate(SIDES):
            nbuf[s, i] = n[p * size : (p + 1) * size].astype(BF16)
        own[s] = n[REACH * size : (REACH + 1) * size]

    def patch_sum(s):
        total = own[s]
        for i in range(len(SIDES)):
            part_a(i, s).wait_recv()
            total = total + recva[s, i].astype(F32)
        return total

    pl.semaphore_wait(barrier, len(SIDES) + n_band - 1)
    for i in range(len(SIDES)):
        weight_a(i).start()

    def step(s, carry):
        compute(s)
        for i in range(len(SIDES)):
            part_a(i, s).start()

        @pl.when(s == 1)
        def _():
            total = wbuf[REACH]
            for i in range(len(SIDES)):
                weight_a(i).wait_recv()
                total = total + wrecva[i]
            wsum[...] = total
            for d in range(1, n_band):
                weight_b(d).start()

        @pl.when(s >= 2)
        def _():
            sumb[s - 2] = patch_sum(s - 2).astype(BF16)
            part_b(s - 2).start()

        return carry

    lax.fori_loop(0, n_band, step, 0)
    sumb[n_band - 2] = patch_sum(n_band - 2).astype(BF16)
    part_b(n_band - 2).start()
    total = patch_sum(n_band - 1)
    weights = wsum[...]
    for d in range(1, n_band):
        weight_b(d).wait_recv()
        weights = weights + wrecvb[d - 1]
    weights = jnp.maximum(weights, 1.0)
    for s in range(n_band - 1):
        part_b(s).wait_recv()
        total = total + recvb[s].astype(F32)
    detection = jnp.zeros((block, PW), F32)
    for b in range(BANDS):
        coadd = total[b * block : (b + 1) * block] / weights[b : b + 1]
        out_ref[b] = coadd
        detection = detection + bw_s[b] * coadd
    det_ref[...] = detection

    for i in range(len(SIDES)):
        weight_a(i).wait_send()
    for d in range(1, n_band):
        weight_b(d).wait_send()

    def drain(s, carry):
        for i in range(len(SIDES)):
            part_a(i, s).wait_send()

        @pl.when(s < n_band - 1)
        def _():
            part_b(s).wait_send()

        return carry

    lax.fori_loop(0, n_band, drain, 0)


def solution(mesh):
    n_ra, n_band = mesh.shape["ra"], mesh.shape["band"]

    def local(
        tiles,
        tile_patch,
        tile_offset,
        tile_weight,
        visit_band,
        coeff_index,
        coeff_table,
        row_kernels,
        column_kernels,
        band_weight,
    ):
        count, rows, width = tiles.shape
        basis = row_kernels.shape[0]
        block = rows // n_band
        size = BANDS * block
        sides = len(SIDES)
        smem = pl.BlockSpec(memory_space=pltpu.SMEM)
        vmem = pl.BlockSpec(memory_space=pltpu.VMEM)

        def body(*refs):
            kernel(n_ra, n_band, *refs)

        return pl.pallas_call(
            body,
            name="coadd",
            out_shape=(
                jax.ShapeDtypeStruct((BANDS, block, PW), F32),
                jax.ShapeDtypeStruct((block, PW), F32),
            ),
            in_specs=[smem] * 6 + [vmem] * 4,
            out_specs=(vmem, vmem),
            scratch_shapes=[
                pltpu.VMEM((24, width), F32),
                pltpu.VMEM((basis * block, width), F32),
                pltpu.VMEM((basis * width, width), BF16),
                pltpu.VMEM((count * block, basis * width), BF16),
                pltpu.VMEM((count * block, width), F32),
                pltpu.VMEM((count * block, PW), BF16),
                pltpu.VMEM((SPREAD * size, count * block), BF16),
                pltpu.VMEM((n_band, sides, size, PW), BF16),
                pltpu.VMEM((n_band, size, PW), F32),
                pltpu.VMEM((n_band, sides, size, PW), BF16),
                pltpu.VMEM((n_band, size, PW), BF16),
                pltpu.VMEM((n_band, size, PW), BF16),
                pltpu.VMEM((SPREAD, block, PW), F32),
                pltpu.VMEM((sides, block, PW), F32),
                pltpu.VMEM((block, PW), F32),
                pltpu.VMEM((n_band - 1, block, PW), F32),
                pltpu.SemaphoreType.DMA((n_band, sides)),
                pltpu.SemaphoreType.DMA((n_band, sides)),
                pltpu.SemaphoreType.DMA((n_band,)),
                pltpu.SemaphoreType.DMA((n_band,)),
                pltpu.SemaphoreType.DMA((sides,)),
                pltpu.SemaphoreType.DMA((sides,)),
                pltpu.SemaphoreType.DMA((n_band - 1,)),
                pltpu.SemaphoreType.DMA((n_band - 1,)),
            ],
            compiler_params=pltpu.CompilerParams(
                collective_id=0, has_side_effects=True, vmem_limit_bytes=48 * 1024 * 1024
            ),
        )(
            tile_patch,
            tile_offset,
            visit_band,
            coeff_index,
            band_weight,
            coeff_table,
            tiles,
            tile_weight.reshape(1, count),
            row_kernels,
            column_kernels,
        )

    return jax.shard_map(
        local,
        mesh=mesh,
        in_specs=(
            P(("ra", "band"), None, None),
            P(("ra", "band")),
            P(("ra", "band")),
            P(("ra", "band")),
            P(("ra", "band")),
            P(("ra", "band")),
            P(),
            P(),
            P(),
            P(),
        ),
        out_specs=(P(None, "band", "ra"), P("band", "ra")),
        check_vma=False,
    )
```

```python
import jax
import jax.numpy as jnp
from jax import lax
from jax.experimental import pallas as pl
from jax.experimental.pallas import tpu as pltpu
from jax.sharding import PartitionSpec as P

PW = 256
BANDS = 6
REACH = 2
SPREAD = 2 * REACH + 1
NB = 2
F32 = jnp.float32
BF16 = jnp.bfloat16
MESH = pl.DeviceIdType.MESH
SIDES = [p for p in range(SPREAD) if p != REACH]


def kernel(
    n_ra,
    n_band,
    patch_s,
    off_s,
    vband_s,
    cidx_s,
    bw_s,
    ctab_s,
    tiles_hbm,
    wt,
    rowk,
    colk,
    out_ref,
    det_ref,
    tiles,
    tile_sem,
    kpad,
    rbase,
    cst,
    ps,
    mat,
    placed,
    a8,
    nbuf,
    own,
    recva,
    sumb,
    recvb,
    wbuf,
    wrecva,
    wsum,
    wrecvb,
    send_a,
    recv_a,
    send_b,
    recv_b,
    wsend_a,
    wrecv_a,
    wsend_b,
    wrecv_b,
):
    me_ra = lax.axis_index("ra")
    me_band = lax.axis_index("band")
    fetch = pltpu.make_async_copy(tiles_hbm, tiles, tile_sem)
    fetch.start()
    count, rows, width = tiles.shape
    basis, taps = rowk.shape
    half = taps // 2
    block = rows // n_band
    per_visit = count // vband_s.shape[0]

    def ra_at(distance):
        return lax.rem(me_ra + distance + n_ra, n_ra)

    def band_at(distance):
        return lax.rem(me_band + distance, n_band)

    barrier = pltpu.get_barrier_semaphore()
    for p in SIDES:
        pl.semaphore_signal(
            barrier, inc=1, device_id=(ra_at(p - REACH), me_band), device_id_type=MESH
        )
    for d in range(1, n_band):
        pl.semaphore_signal(
            barrier, inc=1, device_id=(me_ra, band_at(d)), device_id_type=MESH
        )

    lane = lax.broadcasted_iota(jnp.int32, (block, width), 1)
    sub = lax.broadcasted_iota(jnp.int32, (block, width), 0)
    kpad[...] = jnp.zeros_like(kpad)
    kpad[0:basis, 0:taps] = rowk[...].astype(F32)
    for k in range(basis):
        row = jnp.broadcast_to(kpad[k : k + 1, :], (block, width))
        rbase[k * block : (k + 1) * block, :] = pltpu.roll(
            row, width - half, 1, stride=1, stride_axis=0
        )
    kpad[0:basis, 0:taps] = colk[...].astype(F32)
    flip_r = lax.broadcasted_iota(jnp.int32, (width, width), 0)
    flip_c = lax.broadcasted_iota(jnp.int32, (width, width), 1)
    flip = jnp.where(flip_r + flip_c == taps - 1, 1.0, 0.0).astype(BF16)
    kpad[...] = jnp.dot(kpad[...].astype(BF16), flip, preferred_element_type=F32)

    for k in range(basis):
        row = jnp.broadcast_to(kpad[k : k + 1, :], (block, width))
        base = pltpu.roll(row, width - half, 1, stride=1, stride_axis=0)
        for c in range(0, width, 2 * block):
            parts = []
            for at in (c, c + block):
                part = base if at == 0 else pltpu.roll(base, at, 1)
                if at < half or at + block > width - half:
                    part = jnp.where(jnp.abs(lane - sub - at) <= half, part, 0.0)
                parts.append(part)
            cst[k * width + c : k * width + c + 2 * block, :] = jnp.concatenate(parts, axis=0).astype(BF16)

    spread_r = lax.broadcasted_iota(jnp.int32, (count, count * block), 0)
    spread_c = lax.broadcasted_iota(jnp.int32, (count, count * block), 1)
    spread = jnp.where(spread_c // block == spread_r, 1.0, 0.0).astype(BF16)
    w_lane = jnp.dot(
        jnp.broadcast_to(wt[...], (block, count)), spread, preferred_element_type=F32
    )
    lane8 = lax.broadcasted_iota(jnp.int32, (block, count * block), 1)
    sub8 = lax.broadcasted_iota(jnp.int32, (block, count * block), 0)
    bucket = jnp.zeros((block, count * block), jnp.int32)
    band = jnp.zeros((block, count * block), jnp.int32)
    for j in range(count):
        here = lane8 // block == j
        bucket = jnp.where(here, patch_s[j], bucket)
        band = jnp.where(here, vband_s[j // per_visit], band)
    bucket = bucket - me_ra + REACH
    bucket = jnp.where(bucket < 0, bucket + n_ra, bucket)
    bucket = jnp.where(bucket >= n_ra, bucket - n_ra, bucket)
    diag = lax.rem(lane8, block) == sub8
    for p in range(SPREAD):
        for b in range(0, BANDS, 2):
            parts = [
                jnp.where((bucket == p) & (band == b + h) & diag, w_lane, 0.0) for h in (0, 1)
            ]
            at = (p * BANDS + b) * block
            a8[at : at + 2 * block, :] = jnp.concatenate(parts, axis=0).astype(BF16)
    first = lax.rem(lane8, block) == 0
    aw = jnp.concatenate(
        [
            jnp.where((bucket == p) & (band == sub8) & first, w_lane, 0.0)
            for p in range(SPREAD)
        ]
        + [jnp.zeros((block, count * block), F32)],
        axis=0,
    ).astype(BF16)

    for jp in range(count // 2):
        left, right = [], []
        for h in (0, 1):
            off = off_s[2 * jp + h]
            left.append(jnp.where(lane >= off, 1.0, 0.0))
            right.append(jnp.where(lane < off, 1.0, 0.0))
        at = jp * 2 * block
        placed[at : at + 2 * block, 0:width] = jnp.concatenate(left, axis=0).astype(BF16)
        placed[at : at + 2 * block, width : 2 * width] = jnp.concatenate(right, axis=0).astype(BF16)
    sums = jnp.dot(aw, placed[...], preferred_element_type=F32)
    for p in range(SPREAD):
        wbuf[p] = sums[p * block : (p + 1) * block]

    def weight_a(i):
        p = SIDES[i]
        return pltpu.make_async_remote_copy(
            src_ref=wbuf.at[p],
            dst_ref=wrecva.at[i],
            send_sem=wsend_a.at[i],
            recv_sem=wrecv_a.at[i],
            device_id=(ra_at(p - REACH), me_band),
            device_id_type=MESH,
        )

    def weight_b(d):
        return pltpu.make_async_remote_copy(
            src_ref=wsum,
            dst_ref=wrecvb.at[d - 1],
            send_sem=wsend_b.at[d - 1],
            recv_sem=wrecv_b.at[d - 1],
            device_id=(me_ra, band_at(d)),
            device_id_type=MESH,
        )

    def part_a(i, s):
        p = SIDES[i]
        return pltpu.make_async_remote_copy(
            src_ref=nbuf.at[s, i],
            dst_ref=recva.at[s, i],
            send_sem=send_a.at[s, i],
            recv_sem=recv_a.at[s, i],
            device_id=(ra_at(p - REACH), me_band),
            device_id_type=MESH,
        )

    def part_b(s):
        return pltpu.make_async_remote_copy(
            src_ref=sumb.at[s],
            dst_ref=recvb.at[s],
            send_sem=send_b.at[s],
            recv_sem=recv_b.at[s],
            device_id=(me_ra, band_at(s + 1)),
            device_id_type=MESH,
        )

    def compute(t):
        parts = []
        for h in range(NB):
            r = lax.rem(me_band + 1 + NB * t + h, n_band)
            parts.append(pltpu.roll(rbase[...], r * block, 1))
        lhs = jnp.concatenate(
            [
                parts[h][k * block : (k + 1) * block, 0:rows]
                for k in range(basis)
                for h in range(NB)
            ],
            axis=0,
        ).astype(BF16)
        tall = NB * block
        for jp in range(count // 2):
            t2 = jnp.concatenate([tiles[2 * jp], tiles[2 * jp + 1]], axis=1)
            x = jnp.dot(lhs, t2, preferred_element_type=F32)
            for i in (0, 1):
                j = 2 * jp + i
                c = cidx_s[j]
                for k in range(basis):
                    y = x[k * tall : (k + 1) * tall, i * width : (i + 1) * width] * ctab_s[k, c]
                    ps[j * tall : (j + 1) * tall, k * width : (k + 1) * width] = y.astype(BF16)
        mat[...] = jnp.dot(ps[...], cst[...], preferred_element_type=F32)
        size = BANDS * block
        for h in range(NB):
            for jp in range(count // 2):
                left, right = [], []
                for j in (2 * jp, 2 * jp + 1):
                    off = off_s[j]
                    at = j * tall + h * block
                    moved = pltpu.roll(mat[at : at + block, :], off, 1)
                    left.append(jnp.where(lane >= off, moved, 0.0))
                    right.append(jnp.where(lane < off, moved, 0.0))
                at = jp * 2 * block
                placed[at : at + 2 * block, 0:width] = jnp.concatenate(left, axis=0).astype(BF16)
                placed[at : at + 2 * block, width : 2 * width] = jnp.concatenate(
                    right, axis=0
                ).astype(BF16)
            n = jnp.dot(a8[...], placed[...], preferred_element_type=F32)
            for i, p in enumerate(SIDES):
                nbuf[NB * t + h, i] = n[p * size : (p + 1) * size].astype(BF16)
            own[NB * t + h] = n[REACH * size : (REACH + 1) * size]

    def patch_sum(s):
        total = own[s]
        for i in range(len(SIDES)):
            part_a(i, s).wait_recv()
            total = total + recva[s, i].astype(F32)
        return total

    fetch.wait()
    pl.semaphore_wait(barrier, len(SIDES) + n_band - 1)
    for i in range(len(SIDES)):
        weight_a(i).start()

    def step(t, carry):
        compute(t)
        for h in range(NB):
            for i in range(len(SIDES)):
                part_a(i, NB * t + h).start()

        @pl.when(t == 1)
        def _():
            total = wbuf[REACH]
            for i in range(len(SIDES)):
                weight_a(i).wait_recv()
                total = total + wrecva[i]
            wsum[...] = total
            for d in range(1, n_band):
                weight_b(d).start()

        @pl.when(t >= 1)
        def _():
            for h in range(NB):
                s = NB * t - NB + h
                sumb[s] = patch_sum(s).astype(BF16)
                part_b(s).start()

        return carry

    lax.fori_loop(0, n_band // NB, step, 0)
    for s in range(n_band - NB, n_band - 2):
        sumb[s] = patch_sum(s).astype(BF16)
        part_b(s).start()
    sumb[n_band - 2] = patch_sum(n_band - 2).astype(BF16)
    part_b(n_band - 2).start()
    total = patch_sum(n_band - 1)
    weights = wsum[...]
    for d in range(1, n_band):
        weight_b(d).wait_recv()
        weights = weights + wrecvb[d - 1]
    weights = jnp.maximum(weights, 1.0)
    for s in range(n_band - 1):
        part_b(s).wait_recv()
        total = total + recvb[s].astype(F32)
    detection = jnp.zeros((block, PW), F32)
    for b in range(BANDS):
        coadd = total[b * block : (b + 1) * block] / weights[b : b + 1]
        out_ref[b] = coadd
        detection = detection + bw_s[b] * coadd
    det_ref[...] = detection

    for i in range(len(SIDES)):
        weight_a(i).wait_send()
    for d in range(1, n_band):
        weight_b(d).wait_send()

    def drain(s, carry):
        for i in range(len(SIDES)):
            part_a(i, s).wait_send()

        @pl.when(s < n_band - 1)
        def _():
            part_b(s).wait_send()

        return carry

    lax.fori_loop(0, n_band, drain, 0)


def solution(mesh):
    n_ra, n_band = mesh.shape["ra"], mesh.shape["band"]

    def local(
        tiles,
        tile_patch,
        tile_offset,
        tile_weight,
        visit_band,
        coeff_index,
        coeff_table,
        row_kernels,
        column_kernels,
        band_weight,
    ):
        count, rows, width = tiles.shape
        basis = row_kernels.shape[0]
        block = rows // n_band
        size = BANDS * block
        sides = len(SIDES)
        smem = pl.BlockSpec(memory_space=pltpu.SMEM)
        vmem = pl.BlockSpec(memory_space=pltpu.VMEM)
        hbm = pl.BlockSpec(memory_space=pltpu.HBM)

        def body(*refs):
            kernel(n_ra, n_band, *refs)

        return pl.pallas_call(
            body,
            name="coadd",
            out_shape=(
                jax.ShapeDtypeStruct((BANDS, block, PW), F32),
                jax.ShapeDtypeStruct((block, PW), F32),
            ),
            in_specs=[smem] * 6 + [hbm] + [vmem] * 3,
            out_specs=(vmem, vmem),
            scratch_shapes=[
                pltpu.VMEM((count, rows, width), BF16),
                pltpu.SemaphoreType.DMA,
                pltpu.VMEM((24, width), F32),
                pltpu.VMEM((basis * block, width), F32),
                pltpu.VMEM((basis * width, width), BF16),
                pltpu.VMEM((NB * count * block, basis * width), BF16),
                pltpu.VMEM((NB * count * block, width), F32),
                pltpu.VMEM((count * block, PW), BF16),
                pltpu.VMEM((SPREAD * size, count * block), BF16),
                pltpu.VMEM((n_band, sides, size, PW), BF16),
                pltpu.VMEM((n_band, size, PW), F32),
                pltpu.VMEM((n_band, sides, size, PW), BF16),
                pltpu.VMEM((n_band, size, PW), BF16),
                pltpu.VMEM((n_band, size, PW), BF16),
                pltpu.VMEM((SPREAD, block, PW), F32),
                pltpu.VMEM((sides, block, PW), F32),
                pltpu.VMEM((block, PW), F32),
                pltpu.VMEM((n_band - 1, block, PW), F32),
                pltpu.SemaphoreType.DMA((n_band, sides)),
                pltpu.SemaphoreType.DMA((n_band, sides)),
                pltpu.SemaphoreType.DMA((n_band,)),
                pltpu.SemaphoreType.DMA((n_band,)),
                pltpu.SemaphoreType.DMA((sides,)),
                pltpu.SemaphoreType.DMA((sides,)),
                pltpu.SemaphoreType.DMA((n_band - 1,)),
                pltpu.SemaphoreType.DMA((n_band - 1,)),
            ],
            compiler_params=pltpu.CompilerParams(
                collective_id=0, has_side_effects=True, vmem_limit_bytes=48 * 1024 * 1024
            ),
        )(
            tile_patch,
            tile_offset,
            visit_band,
            coeff_index,
            band_weight,
            coeff_table.T,
            tiles,
            tile_weight.reshape(1, count),
            row_kernels,
            column_kernels,
        )

    return jax.shard_map(
        local,
        mesh=mesh,
        in_specs=(
            P(("ra", "band"), None, None),
            P(("ra", "band")),
            P(("ra", "band")),
            P(("ra", "band")),
            P(("ra", "band")),
            P(("ra", "band")),
            P(),
            P(),
            P(),
            P(),
        ),
        out_specs=(P(None, "band", "ra"), P("band", "ra")),
        check_vma=False,
    )
```

```python
import jax
import jax.numpy as jnp
from jax import lax
from jax.experimental import pallas as pl
from jax.experimental.pallas import tpu as pltpu
from jax.sharding import PartitionSpec as P

PW = 256
BANDS = 6
REACH = 2
SPREAD = 2 * REACH + 1
NB = 2
VMEM_LIMIT = 60 * 1024 * 1024
F32 = jnp.float32
BF16 = jnp.bfloat16
MESH = pl.DeviceIdType.MESH
SIDES = [p for p in range(SPREAD) if p != REACH]


def kernel(
    n_ra,
    n_band,
    inputs,
    out_ref,
    det_ref,
    held,
    in_sem,
    kpad,
    rbase,
    cst,
    ps,
    mat,
    placed,
    a8,
    nbuf,
    own,
    recva,
    sumb,
    recvb,
    wbuf,
    wrecva,
    wsum,
    wrecvb,
    send_a,
    recv_a,
    send_b,
    recv_b,
    wsend_a,
    wrecv_a,
    wsend_b,
    wrecv_b,
):
    me_ra = lax.axis_index("ra")
    me_band = lax.axis_index("band")
    fetches = [
        pltpu.make_async_copy(src, dst, in_sem.at[i])
        for i, (src, dst) in enumerate(zip(inputs, held))
    ]
    for fetch in fetches:
        fetch.start()
    patch_s, off_s, vband_s, cidx_s, bw_s, ctab_s, rowk, colk, wt, tiles = held
    count, rows, width = tiles.shape
    basis, taps = rowk.shape
    half = taps // 2
    block = rows // n_band
    per_visit = count // vband_s.shape[0]

    def ra_at(distance):
        return lax.rem(me_ra + distance + n_ra, n_ra)

    def band_at(distance):
        return lax.rem(me_band + distance, n_band)

    barrier = pltpu.get_barrier_semaphore()
    for p in SIDES:
        pl.semaphore_signal(
            barrier, inc=1, device_id=(ra_at(p - REACH), me_band), device_id_type=MESH
        )
    for d in range(1, n_band):
        pl.semaphore_signal(
            barrier, inc=1, device_id=(me_ra, band_at(d)), device_id_type=MESH
        )

    for fetch in fetches[:-1]:
        fetch.wait()

    lane = lax.broadcasted_iota(jnp.int32, (block, width), 1)
    sub = lax.broadcasted_iota(jnp.int32, (block, width), 0)
    kpad[...] = jnp.zeros_like(kpad)
    kpad[0:basis, 0:taps] = rowk[...].astype(F32)
    for k in range(basis):
        row = jnp.broadcast_to(kpad[k : k + 1, :], (block, width))
        rbase[k * block : (k + 1) * block, :] = pltpu.roll(
            row, width - half, 1, stride=1, stride_axis=0
        )
    kpad[0:basis, 0:taps] = colk[...].astype(F32)
    flip_r = lax.broadcasted_iota(jnp.int32, (width, width), 0)
    flip_c = lax.broadcasted_iota(jnp.int32, (width, width), 1)
    flip = jnp.where(flip_r + flip_c == taps - 1, 1.0, 0.0).astype(BF16)
    kpad[...] = jnp.dot(kpad[...].astype(BF16), flip, preferred_element_type=F32)

    for k in range(basis):
        row = jnp.broadcast_to(kpad[k : k + 1, :], (block, width))
        base = pltpu.roll(row, width - half, 1, stride=1, stride_axis=0)
        for c in range(0, width, 2 * block):
            parts = []
            for at in (c, c + block):
                part = base if at == 0 else pltpu.roll(base, at, 1)
                if at < half or at + block > width - half:
                    part = jnp.where(jnp.abs(lane - sub - at) <= half, part, 0.0)
                parts.append(part)
            cst[k * width + c : k * width + c + 2 * block, :] = jnp.concatenate(parts, axis=0).astype(BF16)

    spread_r = lax.broadcasted_iota(jnp.int32, (count, count * block), 0)
    spread_c = lax.broadcasted_iota(jnp.int32, (count, count * block), 1)
    spread = jnp.where(spread_c // block == spread_r, 1.0, 0.0).astype(BF16)
    w_lane = jnp.dot(
        jnp.broadcast_to(wt[...], (block, count)), spread, preferred_element_type=F32
    )
    lane8 = lax.broadcasted_iota(jnp.int32, (block, count * block), 1)
    sub8 = lax.broadcasted_iota(jnp.int32, (block, count * block), 0)
    bucket = jnp.zeros((block, count * block), jnp.int32)
    band = jnp.zeros((block, count * block), jnp.int32)
    for j in range(count):
        here = lane8 // block == j
        bucket = jnp.where(here, patch_s[j], bucket)
        band = jnp.where(here, vband_s[j // per_visit], band)
    bucket = bucket - me_ra + REACH
    bucket = jnp.where(bucket < 0, bucket + n_ra, bucket)
    bucket = jnp.where(bucket >= n_ra, bucket - n_ra, bucket)
    diag = lax.rem(lane8, block) == sub8
    for p in range(SPREAD):
        for b in range(0, BANDS, 2):
            parts = [
                jnp.where((bucket == p) & (band == b + h) & diag, w_lane, 0.0) for h in (0, 1)
            ]
            at = (p * BANDS + b) * block
            a8[at : at + 2 * block, :] = jnp.concatenate(parts, axis=0).astype(BF16)
    first = lax.rem(lane8, block) == 0
    aw = jnp.concatenate(
        [
            jnp.where((bucket == p) & (band == sub8) & first, w_lane, 0.0)
            for p in range(SPREAD)
        ]
        + [jnp.zeros((block, count * block), F32)],
        axis=0,
    ).astype(BF16)

    for jp in range(count // 2):
        left, right = [], []
        for h in (0, 1):
            off = off_s[2 * jp + h]
            left.append(jnp.where(lane >= off, 1.0, 0.0))
            right.append(jnp.where(lane < off, 1.0, 0.0))
        at = jp * 2 * block
        placed[at : at + 2 * block, 0:width] = jnp.concatenate(left, axis=0).astype(BF16)
        placed[at : at + 2 * block, width : 2 * width] = jnp.concatenate(right, axis=0).astype(BF16)
    sums = jnp.dot(aw, placed[...], preferred_element_type=F32)
    for p in range(SPREAD):
        wbuf[p] = sums[p * block : (p + 1) * block]

    def weight_a(i):
        p = SIDES[i]
        return pltpu.make_async_remote_copy(
            src_ref=wbuf.at[p],
            dst_ref=wrecva.at[i],
            send_sem=wsend_a.at[i],
            recv_sem=wrecv_a.at[i],
            device_id=(ra_at(p - REACH), me_band),
            device_id_type=MESH,
        )

    def weight_b(d):
        return pltpu.make_async_remote_copy(
            src_ref=wsum,
            dst_ref=wrecvb.at[d - 1],
            send_sem=wsend_b.at[d - 1],
            recv_sem=wrecv_b.at[d - 1],
            device_id=(me_ra, band_at(d)),
            device_id_type=MESH,
        )

    def part_a(i, s):
        p = SIDES[i]
        return pltpu.make_async_remote_copy(
            src_ref=nbuf.at[s, i],
            dst_ref=recva.at[s, i],
            send_sem=send_a.at[s, i],
            recv_sem=recv_a.at[s, i],
            device_id=(ra_at(p - REACH), me_band),
            device_id_type=MESH,
        )

    def part_b(s):
        return pltpu.make_async_remote_copy(
            src_ref=sumb.at[s],
            dst_ref=recvb.at[s],
            send_sem=send_b.at[s],
            recv_sem=recv_b.at[s],
            device_id=(me_ra, band_at(s + 1)),
            device_id_type=MESH,
        )

    def compute(t):
        parts = []
        for h in range(NB):
            r = lax.rem(me_band + 1 + NB * t + h, n_band)
            parts.append(pltpu.roll(rbase[...], r * block, 1))
        lhs = jnp.concatenate(
            [
                parts[h][k * block : (k + 1) * block, 0:rows]
                for k in range(basis)
                for h in range(NB)
            ],
            axis=0,
        ).astype(BF16)
        tall = NB * block
        for jp in range(count // 2):
            t2 = jnp.concatenate([tiles[2 * jp], tiles[2 * jp + 1]], axis=1)
            x = jnp.dot(lhs, t2, preferred_element_type=F32)
            for i in (0, 1):
                j = 2 * jp + i
                c = cidx_s[j]
                for k in range(basis):
                    y = x[k * tall : (k + 1) * tall, i * width : (i + 1) * width] * ctab_s[k, c]
                    ps[j * tall : (j + 1) * tall, k * width : (k + 1) * width] = y.astype(BF16)
        mat[...] = jnp.dot(ps[...], cst[...], preferred_element_type=F32)
        size = BANDS * block
        for h in range(NB):
            for jp in range(count // 2):
                left, right = [], []
                for j in (2 * jp, 2 * jp + 1):
                    off = off_s[j]
                    at = j * tall + h * block
                    moved = pltpu.roll(mat[at : at + block, :], off, 1)
                    left.append(jnp.where(lane >= off, moved, 0.0))
                    right.append(jnp.where(lane < off, moved, 0.0))
                at = jp * 2 * block
                placed[at : at + 2 * block, 0:width] = jnp.concatenate(left, axis=0).astype(BF16)
                placed[at : at + 2 * block, width : 2 * width] = jnp.concatenate(
                    right, axis=0
                ).astype(BF16)
            n = jnp.dot(a8[...], placed[...], preferred_element_type=F32)
            for i, p in enumerate(SIDES):
                nbuf[NB * t + h, i] = n[p * size : (p + 1) * size].astype(BF16)
            own[NB * t + h] = n[REACH * size : (REACH + 1) * size]

    def patch_sum(s):
        total = own[s]
        for i in range(len(SIDES)):
            part_a(i, s).wait_recv()
            total = total + recva[s, i].astype(F32)
        return total

    fetches[-1].wait()
    pl.semaphore_wait(barrier, len(SIDES) + n_band - 1)
    for i in range(len(SIDES)):
        weight_a(i).start()

    def step(t, carry):
        compute(t)
        for h in range(NB):
            for i in range(len(SIDES)):
                part_a(i, NB * t + h).start()

        @pl.when(t == 1)
        def _():
            total = wbuf[REACH]
            for i in range(len(SIDES)):
                weight_a(i).wait_recv()
                total = total + wrecva[i]
            wsum[...] = total
            for d in range(1, n_band):
                weight_b(d).start()

        @pl.when(t >= 1)
        def _():
            for h in range(NB):
                s = NB * t - NB + h
                sumb[s] = patch_sum(s).astype(BF16)
                part_b(s).start()

        return carry

    lax.fori_loop(0, n_band // NB, step, 0)
    for s in range(n_band - NB, n_band - 2):
        sumb[s] = patch_sum(s).astype(BF16)
        part_b(s).start()
    sumb[n_band - 2] = patch_sum(n_band - 2).astype(BF16)
    part_b(n_band - 2).start()
    total = patch_sum(n_band - 1)
    weights = wsum[...]
    for d in range(1, n_band):
        weight_b(d).wait_recv()
        weights = weights + wrecvb[d - 1]
    weights = jnp.maximum(weights, 1.0)
    for s in range(n_band - 1):
        part_b(s).wait_recv()
        total = total + recvb[s].astype(F32)
    detection = jnp.zeros((block, PW), F32)
    for b in range(BANDS):
        coadd = total[b * block : (b + 1) * block] / weights[b : b + 1]
        out_ref[b] = coadd
        detection = detection + bw_s[b] * coadd
    det_ref[...] = detection

    for i in range(len(SIDES)):
        weight_a(i).wait_send()
    for d in range(1, n_band):
        weight_b(d).wait_send()

    def drain(s, carry):
        for i in range(len(SIDES)):
            part_a(i, s).wait_send()

        @pl.when(s < n_band - 1)
        def _():
            part_b(s).wait_send()

        return carry

    lax.fori_loop(0, n_band, drain, 0)


def solution(mesh):
    n_ra, n_band = mesh.shape["ra"], mesh.shape["band"]

    def local(
        tiles,
        tile_patch,
        tile_offset,
        tile_weight,
        visit_band,
        coeff_index,
        coeff_table,
        row_kernels,
        column_kernels,
        band_weight,
    ):
        count, rows, width = tiles.shape
        basis = row_kernels.shape[0]
        block = rows // n_band
        size = BANDS * block
        sides = len(SIDES)
        vmem = pl.BlockSpec(memory_space=pltpu.VMEM)
        hbm = pl.BlockSpec(memory_space=pltpu.HBM)

        arrays = (
            tile_patch,
            tile_offset,
            visit_band,
            coeff_index,
            band_weight,
            coeff_table.T,
            row_kernels,
            column_kernels,
            tile_weight.reshape(1, count),
            tiles,
        )
        spaces = [pltpu.SMEM] * 6 + [pltpu.VMEM] * 4

        def body(*refs):
            n = len(arrays)
            held = refs[n + 2 : 2 * n + 2]
            kernel(n_ra, n_band, refs[:n], *refs[n : n + 2], held, *refs[2 * n + 2 :])

        return pl.pallas_call(
            body,
            name="coadd",
            out_shape=(
                jax.ShapeDtypeStruct((BANDS, block, PW), F32),
                jax.ShapeDtypeStruct((block, PW), F32),
            ),
            in_specs=[hbm] * len(arrays),
            out_specs=(vmem, vmem),
            scratch_shapes=[
                *[space(a.shape, a.dtype) for space, a in zip(spaces, arrays)],
                pltpu.SemaphoreType.DMA((len(arrays),)),
                pltpu.VMEM((24, width), F32),
                pltpu.VMEM((basis * block, width), F32),
                pltpu.VMEM((basis * width, width), BF16),
                pltpu.VMEM((NB * count * block, basis * width), BF16),
                pltpu.VMEM((NB * count * block, width), F32),
                pltpu.VMEM((count * block, PW), BF16),
                pltpu.VMEM((SPREAD * size, count * block), BF16),
                pltpu.VMEM((n_band, sides, size, PW), BF16),
                pltpu.VMEM((n_band, size, PW), F32),
                pltpu.VMEM((n_band, sides, size, PW), BF16),
                pltpu.VMEM((n_band, size, PW), BF16),
                pltpu.VMEM((n_band, size, PW), BF16),
                pltpu.VMEM((SPREAD, block, PW), F32),
                pltpu.VMEM((sides, block, PW), F32),
                pltpu.VMEM((block, PW), F32),
                pltpu.VMEM((n_band - 1, block, PW), F32),
                pltpu.SemaphoreType.DMA((n_band, sides)),
                pltpu.SemaphoreType.DMA((n_band, sides)),
                pltpu.SemaphoreType.DMA((n_band,)),
                pltpu.SemaphoreType.DMA((n_band,)),
                pltpu.SemaphoreType.DMA((sides,)),
                pltpu.SemaphoreType.DMA((sides,)),
                pltpu.SemaphoreType.DMA((n_band - 1,)),
                pltpu.SemaphoreType.DMA((n_band - 1,)),
            ],
            compiler_params=pltpu.CompilerParams(
                collective_id=0, has_side_effects=True, vmem_limit_bytes=VMEM_LIMIT
            ),
        )(*arrays)

    return jax.shard_map(
        local,
        mesh=mesh,
        in_specs=(
            P(("ra", "band"), None, None),
            P(("ra", "band")),
            P(("ra", "band")),
            P(("ra", "band")),
            P(("ra", "band")),
            P(("ra", "band")),
            P(),
            P(),
            P(),
            P(),
        ),
        out_specs=(P(None, "band", "ra"), P("band", "ra")),
        check_vma=False,
    )
```

```python
import jax
import jax.numpy as jnp
from jax import lax
from jax.experimental import pallas as pl
from jax.experimental.pallas import tpu as pltpu
from jax.sharding import PartitionSpec as P

PW = 256
BANDS = 6
REACH = 2
SPREAD = 2 * REACH + 1
NB = 2
LAG = 2
VMEM_LIMIT = 60 * 1024 * 1024
F32 = jnp.float32
BF16 = jnp.bfloat16
MESH = pl.DeviceIdType.MESH
SIDES = [p for p in range(SPREAD) if p != REACH]


def kernel(
    n_ra,
    n_band,
    inputs,
    out_ref,
    det_ref,
    held,
    in_sem,
    kpad,
    rbase,
    cst,
    ps,
    mat,
    placed,
    a8,
    nbuf,
    own,
    recva,
    sumb,
    recvb,
    wbuf,
    wrecva,
    wsum,
    wrecvb,
    send_a,
    recv_a,
    send_b,
    recv_b,
    wsend_a,
    wrecv_a,
    wsend_b,
    wrecv_b,
):
    me_ra = lax.axis_index("ra")
    me_band = lax.axis_index("band")
    fetches = [
        pltpu.make_async_copy(src, dst, in_sem.at[i])
        for i, (src, dst) in enumerate(zip(inputs, held))
    ]
    for fetch in fetches:
        fetch.start()
    patch_s, off_s, vband_s, cidx_s, bw_s, ctab_s, rowk, colk, wt, tiles = held
    count, rows, width = tiles.shape
    basis, taps = rowk.shape
    half = taps // 2
    block = rows // n_band
    per_visit = count // vband_s.shape[0]

    def ra_at(distance):
        return lax.rem(me_ra + distance + n_ra, n_ra)

    def band_at(distance):
        return lax.rem(me_band + distance, n_band)

    barrier = pltpu.get_barrier_semaphore()
    for p in SIDES:
        pl.semaphore_signal(
            barrier, inc=1, device_id=(ra_at(p - REACH), me_band), device_id_type=MESH
        )
    for d in range(1, n_band):
        pl.semaphore_signal(
            barrier, inc=1, device_id=(me_ra, band_at(d)), device_id_type=MESH
        )

    for fetch in fetches[:-1]:
        fetch.wait()

    lane = lax.broadcasted_iota(jnp.int32, (block, width), 1)
    sub = lax.broadcasted_iota(jnp.int32, (block, width), 0)
    kpad[...] = jnp.zeros_like(kpad)
    kpad[0:basis, 0:taps] = rowk[...].astype(F32)
    for k in range(basis):
        row = jnp.broadcast_to(kpad[k : k + 1, :], (block, width))
        rbase[k * block : (k + 1) * block, :] = pltpu.roll(
            row, width - half, 1, stride=1, stride_axis=0
        )
    kpad[0:basis, 0:taps] = colk[...].astype(F32)
    flip_r = lax.broadcasted_iota(jnp.int32, (width, width), 0)
    flip_c = lax.broadcasted_iota(jnp.int32, (width, width), 1)
    flip = jnp.where(flip_r + flip_c == taps - 1, 1.0, 0.0).astype(BF16)
    kpad[...] = jnp.dot(kpad[...].astype(BF16), flip, preferred_element_type=F32)

    for k in range(basis):
        row = jnp.broadcast_to(kpad[k : k + 1, :], (block, width))
        base = pltpu.roll(row, width - half, 1, stride=1, stride_axis=0)
        for c in range(0, width, 2 * block):
            parts = []
            for at in (c, c + block):
                part = base if at == 0 else pltpu.roll(base, at, 1)
                if at < half or at + block > width - half:
                    part = jnp.where(jnp.abs(lane - sub - at) <= half, part, 0.0)
                parts.append(part)
            cst[k * width + c : k * width + c + 2 * block, :] = jnp.concatenate(parts, axis=0).astype(BF16)

    spread_r = lax.broadcasted_iota(jnp.int32, (count, count * block), 0)
    spread_c = lax.broadcasted_iota(jnp.int32, (count, count * block), 1)
    spread = jnp.where(spread_c // block == spread_r, 1.0, 0.0).astype(BF16)
    w_lane = jnp.dot(
        jnp.broadcast_to(wt[...], (block, count)), spread, preferred_element_type=F32
    )
    lane8 = lax.broadcasted_iota(jnp.int32, (block, count * block), 1)
    sub8 = lax.broadcasted_iota(jnp.int32, (block, count * block), 0)
    bucket = jnp.zeros((block, count * block), jnp.int32)
    band = jnp.zeros((block, count * block), jnp.int32)
    for j in range(count):
        here = lane8 // block == j
        bucket = jnp.where(here, patch_s[j], bucket)
        band = jnp.where(here, vband_s[j // per_visit], band)
    bucket = bucket - me_ra + REACH
    bucket = jnp.where(bucket < 0, bucket + n_ra, bucket)
    bucket = jnp.where(bucket >= n_ra, bucket - n_ra, bucket)
    diag = lax.rem(lane8, block) == sub8
    for p in range(SPREAD):
        for b in range(0, BANDS, 2):
            parts = [
                jnp.where((bucket == p) & (band == b + h) & diag, w_lane, 0.0) for h in (0, 1)
            ]
            at = (p * BANDS + b) * block
            a8[at : at + 2 * block, :] = jnp.concatenate(parts, axis=0).astype(BF16)
    first = lax.rem(lane8, block) == 0
    aw = jnp.concatenate(
        [
            jnp.where((bucket == p) & (band == sub8) & first, w_lane, 0.0)
            for p in range(SPREAD)
        ]
        + [jnp.zeros((block, count * block), F32)],
        axis=0,
    ).astype(BF16)

    for jp in range(count // 2):
        left, right = [], []
        for h in (0, 1):
            off = off_s[2 * jp + h]
            left.append(jnp.where(lane >= off, 1.0, 0.0))
            right.append(jnp.where(lane < off, 1.0, 0.0))
        at = jp * 2 * block
        placed[at : at + 2 * block, 0:width] = jnp.concatenate(left, axis=0).astype(BF16)
        placed[at : at + 2 * block, width : 2 * width] = jnp.concatenate(right, axis=0).astype(BF16)
    sums = jnp.dot(aw, placed[...], preferred_element_type=F32)
    for p in range(SPREAD):
        wbuf[p] = sums[p * block : (p + 1) * block]

    def weight_a(i):
        p = SIDES[i]
        return pltpu.make_async_remote_copy(
            src_ref=wbuf.at[p],
            dst_ref=wrecva.at[i],
            send_sem=wsend_a.at[i],
            recv_sem=wrecv_a.at[i],
            device_id=(ra_at(p - REACH), me_band),
            device_id_type=MESH,
        )

    def weight_b(d):
        return pltpu.make_async_remote_copy(
            src_ref=wsum,
            dst_ref=wrecvb.at[d - 1],
            send_sem=wsend_b.at[d - 1],
            recv_sem=wrecv_b.at[d - 1],
            device_id=(me_ra, band_at(d)),
            device_id_type=MESH,
        )

    def part_a(i, s):
        p = SIDES[i]
        return pltpu.make_async_remote_copy(
            src_ref=nbuf.at[s, i],
            dst_ref=recva.at[s, i],
            send_sem=send_a.at[s, i],
            recv_sem=recv_a.at[s, i],
            device_id=(ra_at(p - REACH), me_band),
            device_id_type=MESH,
        )

    def part_b(s):
        return pltpu.make_async_remote_copy(
            src_ref=sumb.at[s],
            dst_ref=recvb.at[s],
            send_sem=send_b.at[s],
            recv_sem=recv_b.at[s],
            device_id=(me_ra, band_at(s + 1)),
            device_id_type=MESH,
        )

    def compute(t):
        parts = []
        for h in range(NB):
            r = lax.rem(me_band + 1 + NB * t + h, n_band)
            parts.append(pltpu.roll(rbase[...], r * block, 1))
        lhs = jnp.concatenate(
            [
                parts[h][k * block : (k + 1) * block, 0:rows]
                for k in range(basis)
                for h in range(NB)
            ],
            axis=0,
        ).astype(BF16)
        tall = NB * block
        for jp in range(count // 2):
            t2 = jnp.concatenate([tiles[2 * jp], tiles[2 * jp + 1]], axis=1)
            x = jnp.dot(lhs, t2, preferred_element_type=F32)
            for i in (0, 1):
                j = 2 * jp + i
                c = cidx_s[j]
                for k in range(basis):
                    y = x[k * tall : (k + 1) * tall, i * width : (i + 1) * width] * ctab_s[k, c]
                    ps[j * tall : (j + 1) * tall, k * width : (k + 1) * width] = y.astype(BF16)
        mat[...] = jnp.dot(ps[...], cst[...], preferred_element_type=F32)
        size = BANDS * block
        for h in range(NB):
            for jp in range(count // 2):
                left, right = [], []
                for j in (2 * jp, 2 * jp + 1):
                    off = off_s[j]
                    at = j * tall + h * block
                    moved = pltpu.roll(mat[at : at + block, :], off, 1)
                    left.append(jnp.where(lane >= off, moved, 0.0))
                    right.append(jnp.where(lane < off, moved, 0.0))
                at = jp * 2 * block
                placed[at : at + 2 * block, 0:width] = jnp.concatenate(left, axis=0).astype(BF16)
                placed[at : at + 2 * block, width : 2 * width] = jnp.concatenate(
                    right, axis=0
                ).astype(BF16)
            n = jnp.dot(a8[...], placed[...], preferred_element_type=F32)
            for i, p in enumerate(SIDES):
                nbuf[NB * t + h, i] = n[p * size : (p + 1) * size].astype(BF16)
            own[NB * t + h] = n[REACH * size : (REACH + 1) * size]

    def patch_sum(s):
        total = own[s]
        for i in range(len(SIDES)):
            part_a(i, s).wait_recv()
            total = total + recva[s, i].astype(F32)
        return total

    fetches[-1].wait()
    def step(t, carry):
        compute(t)

        @pl.when(t == 0)
        def _():
            pl.semaphore_wait(barrier, len(SIDES) + n_band - 1)
            for i in range(len(SIDES)):
                weight_a(i).start()

        for h in range(NB):
            for i in range(len(SIDES)):
                part_a(i, NB * t + h).start()

        @pl.when(t == 2)
        def _():
            total = wbuf[REACH]
            for i in range(len(SIDES)):
                weight_a(i).wait_recv()
                total = total + wrecva[i]
            wsum[...] = total
            for d in range(1, n_band):
                weight_b(d).start()

        @pl.when(t >= LAG)
        def _():
            for h in range(NB):
                s = NB * (t - LAG) + h
                sumb[s] = patch_sum(s).astype(BF16)
                part_b(s).start()

        return carry

    lax.fori_loop(0, n_band // NB, step, 0)
    for s in range(n_band - LAG * NB, n_band - 2):
        sumb[s] = patch_sum(s).astype(BF16)
        part_b(s).start()
    sumb[n_band - 2] = patch_sum(n_band - 2).astype(BF16)
    part_b(n_band - 2).start()
    total = patch_sum(n_band - 1)
    weights = wsum[...]
    for d in range(1, n_band):
        weight_b(d).wait_recv()
        weights = weights + wrecvb[d - 1]
    weights = jnp.maximum(weights, 1.0)
    for s in range(n_band - 1):
        part_b(s).wait_recv()
        total = total + recvb[s].astype(F32)
    detection = jnp.zeros((block, PW), F32)
    for b in range(BANDS):
        coadd = total[b * block : (b + 1) * block] / weights[b : b + 1]
        out_ref[b] = coadd
        detection = detection + bw_s[b] * coadd
    det_ref[...] = detection

    for i in range(len(SIDES)):
        weight_a(i).wait_send()
    for d in range(1, n_band):
        weight_b(d).wait_send()

    def drain(s, carry):
        for i in range(len(SIDES)):
            part_a(i, s).wait_send()

        @pl.when(s < n_band - 1)
        def _():
            part_b(s).wait_send()

        return carry

    lax.fori_loop(0, n_band, drain, 0)


def solution(mesh):
    n_ra, n_band = mesh.shape["ra"], mesh.shape["band"]

    def local(
        tiles,
        tile_patch,
        tile_offset,
        tile_weight,
        visit_band,
        coeff_index,
        coeff_table,
        row_kernels,
        column_kernels,
        band_weight,
    ):
        count, rows, width = tiles.shape
        basis = row_kernels.shape[0]
        block = rows // n_band
        size = BANDS * block
        sides = len(SIDES)
        vmem = pl.BlockSpec(memory_space=pltpu.VMEM)
        hbm = pl.BlockSpec(memory_space=pltpu.HBM)

        arrays = (
            tile_patch,
            tile_offset,
            visit_band,
            coeff_index,
            band_weight,
            coeff_table.T,
            row_kernels,
            column_kernels,
            tile_weight.reshape(1, count),
            tiles,
        )
        spaces = [pltpu.SMEM] * 6 + [pltpu.VMEM] * 4

        def body(*refs):
            n = len(arrays)
            held = refs[n + 2 : 2 * n + 2]
            kernel(n_ra, n_band, refs[:n], *refs[n : n + 2], held, *refs[2 * n + 2 :])

        return pl.pallas_call(
            body,
            name="coadd",
            out_shape=(
                pltpu.VMEM((BANDS, block, PW), F32),
                pltpu.VMEM((block, PW), F32),
            ),
            in_specs=[hbm] * len(arrays),
            out_specs=(vmem, vmem),
            scratch_shapes=[
                *[space(a.shape, a.dtype) for space, a in zip(spaces, arrays)],
                pltpu.SemaphoreType.DMA((len(arrays),)),
                pltpu.VMEM((24, width), F32),
                pltpu.VMEM((basis * block, width), F32),
                pltpu.VMEM((basis * width, width), BF16),
                pltpu.VMEM((NB * count * block, basis * width), BF16),
                pltpu.VMEM((NB * count * block, width), F32),
                pltpu.VMEM((count * block, PW), BF16),
                pltpu.VMEM((SPREAD * size, count * block), BF16),
                pltpu.VMEM((n_band, sides, size, PW), BF16),
                pltpu.VMEM((n_band, size, PW), F32),
                pltpu.VMEM((n_band, sides, size, PW), BF16),
                pltpu.VMEM((n_band, size, PW), BF16),
                pltpu.VMEM((n_band, size, PW), BF16),
                pltpu.VMEM((SPREAD, block, PW), F32),
                pltpu.VMEM((sides, block, PW), F32),
                pltpu.VMEM((block, PW), F32),
                pltpu.VMEM((n_band - 1, block, PW), F32),
                pltpu.SemaphoreType.DMA((n_band, sides)),
                pltpu.SemaphoreType.DMA((n_band, sides)),
                pltpu.SemaphoreType.DMA((n_band,)),
                pltpu.SemaphoreType.DMA((n_band,)),
                pltpu.SemaphoreType.DMA((sides,)),
                pltpu.SemaphoreType.DMA((sides,)),
                pltpu.SemaphoreType.DMA((n_band - 1,)),
                pltpu.SemaphoreType.DMA((n_band - 1,)),
            ],
            compiler_params=pltpu.CompilerParams(
                collective_id=0, has_side_effects=True, vmem_limit_bytes=VMEM_LIMIT
            ),
        )(*arrays)

    return jax.shard_map(
        local,
        mesh=mesh,
        in_specs=(
            P(("ra", "band"), None, None),
            P(("ra", "band")),
            P(("ra", "band")),
            P(("ra", "band")),
            P(("ra", "band")),
            P(("ra", "band")),
            P(),
            P(),
            P(),
            P(),
        ),
        out_specs=(P(None, "band", "ra"), P("band", "ra")),
        check_vma=False,
    )
```

```python
import jax
import jax.numpy as jnp
from jax import lax
from jax.experimental import pallas as pl
from jax.experimental.pallas import tpu as pltpu
from jax.sharding import PartitionSpec as P

PW = 256
BANDS = 6
REACH = 2
SPREAD = 2 * REACH + 1
NB = 2
LAG = 3
VMEM_LIMIT = 60 * 1024 * 1024
F32 = jnp.float32
BF16 = jnp.bfloat16
MESH = pl.DeviceIdType.MESH
SIDES = [0, 4, 1, 3]


def kernel(
    n_ra,
    n_band,
    inputs,
    out_ref,
    det_ref,
    held,
    in_sem,
    kpad,
    rbase,
    cst,
    ps,
    mat,
    placed,
    a8,
    nbuf,
    own,
    recva,
    sumb,
    recvb,
    wbuf,
    wrecva,
    wsum,
    wrecvb,
    send_a,
    recv_a,
    send_b,
    recv_b,
    wsend_a,
    wrecv_a,
    wsend_b,
    wrecv_b,
):
    me_ra = lax.axis_index("ra")
    me_band = lax.axis_index("band")
    fetches = [
        pltpu.make_async_copy(src, dst, in_sem.at[i])
        for i, (src, dst) in enumerate(zip(inputs, held))
    ]
    for fetch in fetches:
        fetch.start()
    patch_s, off_s, vband_s, cidx_s, bw_s, ctab_s, rowk, colk, wt, tiles = held
    count, rows, width = tiles.shape
    basis, taps = rowk.shape
    half = taps // 2
    block = rows // n_band
    per_visit = count // vband_s.shape[0]

    def ra_at(distance):
        return lax.rem(me_ra + distance + n_ra, n_ra)

    def band_at(distance):
        return lax.rem(me_band + distance, n_band)

    barrier = pltpu.get_barrier_semaphore()
    for p in SIDES:
        pl.semaphore_signal(
            barrier, inc=1, device_id=(ra_at(p - REACH), me_band), device_id_type=MESH
        )
    for d in range(1, n_band):
        pl.semaphore_signal(
            barrier, inc=1, device_id=(me_ra, band_at(d)), device_id_type=MESH
        )

    for fetch in fetches[:-1]:
        fetch.wait()

    lane = lax.broadcasted_iota(jnp.int32, (block, width), 1)
    sub = lax.broadcasted_iota(jnp.int32, (block, width), 0)
    kpad[...] = jnp.zeros_like(kpad)
    kpad[0:basis, 0:taps] = rowk[...].astype(F32)
    for k in range(basis):
        row = jnp.broadcast_to(kpad[k : k + 1, :], (block, width))
        rbase[k * block : (k + 1) * block, :] = pltpu.roll(
            row, width - half, 1, stride=1, stride_axis=0
        )
    kpad[0:basis, 0:taps] = colk[...].astype(F32)
    flip_r = lax.broadcasted_iota(jnp.int32, (width, width), 0)
    flip_c = lax.broadcasted_iota(jnp.int32, (width, width), 1)
    flip = jnp.where(flip_r + flip_c == taps - 1, 1.0, 0.0).astype(BF16)
    kpad[...] = jnp.dot(kpad[...].astype(BF16), flip, preferred_element_type=F32)

    for k in range(basis):
        row = jnp.broadcast_to(kpad[k : k + 1, :], (block, width))
        base = pltpu.roll(row, width - half, 1, stride=1, stride_axis=0)
        for c in range(0, width, 2 * block):
            parts = []
            for at in (c, c + block):
                part = base if at == 0 else pltpu.roll(base, at, 1)
                if at < half or at + block > width - half:
                    part = jnp.where(jnp.abs(lane - sub - at) <= half, part, 0.0)
                parts.append(part)
            cst[k * width + c : k * width + c + 2 * block, :] = jnp.concatenate(parts, axis=0).astype(BF16)

    spread_r = lax.broadcasted_iota(jnp.int32, (count, count * block), 0)
    spread_c = lax.broadcasted_iota(jnp.int32, (count, count * block), 1)
    spread = jnp.where(spread_c // block == spread_r, 1.0, 0.0).astype(BF16)
    w_lane = jnp.dot(
        jnp.broadcast_to(wt[...], (block, count)), spread, preferred_element_type=F32
    )
    lane8 = lax.broadcasted_iota(jnp.int32, (block, count * block), 1)
    sub8 = lax.broadcasted_iota(jnp.int32, (block, count * block), 0)
    bucket = jnp.zeros((block, count * block), jnp.int32)
    band = jnp.zeros((block, count * block), jnp.int32)
    for j in range(count):
        here = lane8 // block == j
        bucket = jnp.where(here, patch_s[j], bucket)
        band = jnp.where(here, vband_s[j // per_visit], band)
    bucket = bucket - me_ra + REACH
    bucket = jnp.where(bucket < 0, bucket + n_ra, bucket)
    bucket = jnp.where(bucket >= n_ra, bucket - n_ra, bucket)
    diag = lax.rem(lane8, block) == sub8
    for p in range(SPREAD):
        for b in range(0, BANDS, 2):
            parts = [
                jnp.where((bucket == p) & (band == b + h) & diag, w_lane, 0.0) for h in (0, 1)
            ]
            at = (p * BANDS + b) * block
            a8[at : at + 2 * block, :] = jnp.concatenate(parts, axis=0).astype(BF16)
    first = lax.rem(lane8, block) == 0
    aw = jnp.concatenate(
        [
            jnp.where((bucket == p) & (band == sub8) & first, w_lane, 0.0)
            for p in range(SPREAD)
        ]
        + [jnp.zeros((block, count * block), F32)],
        axis=0,
    ).astype(BF16)

    for jp in range(count // 2):
        left, right = [], []
        for h in (0, 1):
            off = off_s[2 * jp + h]
            left.append(jnp.where(lane >= off, 1.0, 0.0))
            right.append(jnp.where(lane < off, 1.0, 0.0))
        at = jp * 2 * block
        placed[at : at + 2 * block, 0:width] = jnp.concatenate(left, axis=0).astype(BF16)
        placed[at : at + 2 * block, width : 2 * width] = jnp.concatenate(right, axis=0).astype(BF16)
    sums = jnp.dot(aw, placed[:, 0:PW], preferred_element_type=F32)
    for p in range(SPREAD):
        wbuf[p] = sums[p * block : (p + 1) * block]

    def weight_a(i):
        p = SIDES[i]
        return pltpu.make_async_remote_copy(
            src_ref=wbuf.at[p],
            dst_ref=wrecva.at[i],
            send_sem=wsend_a.at[i],
            recv_sem=wrecv_a.at[i],
            device_id=(ra_at(p - REACH), me_band),
            device_id_type=MESH,
        )

    def weight_b(d):
        return pltpu.make_async_remote_copy(
            src_ref=wsum,
            dst_ref=wrecvb.at[d - 1],
            send_sem=wsend_b.at[d - 1],
            recv_sem=wrecv_b.at[d - 1],
            device_id=(me_ra, band_at(d)),
            device_id_type=MESH,
        )

    def part_a(i, s):
        p = SIDES[i]
        return pltpu.make_async_remote_copy(
            src_ref=nbuf.at[s, i],
            dst_ref=recva.at[s, i],
            send_sem=send_a.at[s, i],
            recv_sem=recv_a.at[s, i],
            device_id=(ra_at(p - REACH), me_band),
            device_id_type=MESH,
        )

    def part_b(s):
        return pltpu.make_async_remote_copy(
            src_ref=sumb.at[s],
            dst_ref=recvb.at[s],
            send_sem=send_b.at[s],
            recv_sem=recv_b.at[s],
            device_id=(me_ra, band_at(s + 1)),
            device_id_type=MESH,
        )

    def compute(t):
        parts = []
        for h in range(NB):
            r = lax.rem(me_band + 1 + NB * t + h, n_band)
            parts.append(pltpu.roll(rbase[...], r * block, 1))
        lhs = jnp.concatenate(
            [
                parts[h][k * block : (k + 1) * block, 0:rows]
                for k in range(basis)
                for h in range(NB)
            ],
            axis=0,
        ).astype(BF16)
        tall = NB * block
        for jp in range(count // 2):
            t2 = jnp.concatenate([tiles[2 * jp], tiles[2 * jp + 1]], axis=1)
            x = jnp.dot(lhs, t2, preferred_element_type=F32)
            for i in (0, 1):
                j = 2 * jp + i
                c = cidx_s[j]
                for k in range(basis):
                    y = x[k * tall : (k + 1) * tall, i * width : (i + 1) * width] * ctab_s[k, c]
                    ps[j * tall : (j + 1) * tall, k * width : (k + 1) * width] = y.astype(BF16)
        mat[...] = jnp.dot(ps[...], cst[...], preferred_element_type=F32)
        size = BANDS * block
        for h in range(NB):
            for jp in range(count // 2):
                left, right = [], []
                for j in (2 * jp, 2 * jp + 1):
                    off = off_s[j]
                    at = j * tall + h * block
                    moved = pltpu.roll(mat[at : at + block, :], off, 1)
                    left.append(jnp.where(lane >= off, moved, 0.0))
                    right.append(jnp.where(lane < off, moved, 0.0))
                at = jp * 2 * block
                for part, q in ((left, h * PW), (right, h * PW + width)):
                    placed[at : at + 2 * block, q : q + width] = jnp.concatenate(
                        part, axis=0
                    ).astype(BF16)
        n = jnp.dot(a8[...], placed[...], preferred_element_type=F32)
        for h in range(NB):
            here = n[:, h * PW : (h + 1) * PW]
            for i, p in enumerate(SIDES):
                nbuf[NB * t + h, i] = here[p * size : (p + 1) * size].astype(BF16)
            own[NB * t + h] = here[REACH * size : (REACH + 1) * size]

    def patch_sum(s):
        total = own[s]
        for i in range(len(SIDES)):
            part_a(i, s).wait_recv()
            total = total + recva[s, i].astype(F32)
        return total

    fetches[-1].wait()
    def step(t, carry):
        compute(t)

        @pl.when(t == 0)
        def _():
            pl.semaphore_wait(barrier, len(SIDES) + n_band - 1)
            for i in range(len(SIDES)):
                weight_a(i).start()

        for h in range(NB):
            for i in range(len(SIDES)):
                part_a(i, NB * t + h).start()

        @pl.when(t == 2)
        def _():
            total = wbuf[REACH]
            for i in range(len(SIDES)):
                weight_a(i).wait_recv()
                total = total + wrecva[i]
            wsum[...] = total
            for d in range(1, n_band):
                weight_b(d).start()

        @pl.when(t >= LAG)
        def _():
            for h in range(NB):
                s = NB * (t - LAG) + h
                sumb[s] = patch_sum(s).astype(BF16)
                part_b(s).start()

        return carry

    lax.fori_loop(0, n_band // NB, step, 0)
    for s in range(n_band - LAG * NB, n_band - 2):
        sumb[s] = patch_sum(s).astype(BF16)
        part_b(s).start()
    sumb[n_band - 2] = patch_sum(n_band - 2).astype(BF16)
    part_b(n_band - 2).start()
    total = patch_sum(n_band - 1)
    weights = wsum[...]
    for d in range(1, n_band):
        weight_b(d).wait_recv()
        weights = weights + wrecvb[d - 1]
    weights = jnp.maximum(weights, 1.0)
    for s in range(n_band - 1):
        part_b(s).wait_recv()
        total = total + recvb[s].astype(F32)
    detection = jnp.zeros((block, PW), F32)
    for b in range(BANDS):
        coadd = total[b * block : (b + 1) * block] / weights[b : b + 1]
        out_ref[b] = coadd
        detection = detection + bw_s[b] * coadd
    det_ref[...] = detection

    for i in range(len(SIDES)):
        weight_a(i).wait_send()
    for d in range(1, n_band):
        weight_b(d).wait_send()

    def drain(s, carry):
        for i in range(len(SIDES)):
            part_a(i, s).wait_send()

        @pl.when(s < n_band - 1)
        def _():
            part_b(s).wait_send()

        return carry

    lax.fori_loop(0, n_band, drain, 0)


def solution(mesh):
    n_ra, n_band = mesh.shape["ra"], mesh.shape["band"]

    def local(
        tiles,
        tile_patch,
        tile_offset,
        tile_weight,
        visit_band,
        coeff_index,
        coeff_table,
        row_kernels,
        column_kernels,
        band_weight,
    ):
        count, rows, width = tiles.shape
        basis = row_kernels.shape[0]
        block = rows // n_band
        size = BANDS * block
        sides = len(SIDES)
        vmem = pl.BlockSpec(memory_space=pltpu.VMEM)
        hbm = pl.BlockSpec(memory_space=pltpu.HBM)

        arrays = (
            tile_patch,
            tile_offset,
            visit_band,
            coeff_index,
            band_weight,
            coeff_table.T,
            row_kernels,
            column_kernels,
            tile_weight.reshape(1, count),
            tiles,
        )
        spaces = [pltpu.SMEM] * 6 + [pltpu.VMEM] * 4

        def body(*refs):
            n = len(arrays)
            held = refs[n + 2 : 2 * n + 2]
            kernel(n_ra, n_band, refs[:n], *refs[n : n + 2], held, *refs[2 * n + 2 :])

        return pl.pallas_call(
            body,
            name="coadd",
            out_shape=(
                pltpu.VMEM((BANDS, block, PW), F32),
                pltpu.VMEM((block, PW), F32),
            ),
            in_specs=[hbm] * len(arrays),
            out_specs=(vmem, vmem),
            scratch_shapes=[
                *[space(a.shape, a.dtype) for space, a in zip(spaces, arrays)],
                pltpu.SemaphoreType.DMA((len(arrays),)),
                pltpu.VMEM((24, width), F32),
                pltpu.VMEM((basis * block, width), F32),
                pltpu.VMEM((basis * width, width), BF16),
                pltpu.VMEM((NB * count * block, basis * width), BF16),
                pltpu.VMEM((NB * count * block, width), F32),
                pltpu.VMEM((count * block, NB * PW), BF16),
                pltpu.VMEM((SPREAD * size, count * block), BF16),
                pltpu.VMEM((n_band, sides, size, PW), BF16),
                pltpu.VMEM((n_band, size, PW), F32),
                pltpu.VMEM((n_band, sides, size, PW), BF16),
                pltpu.VMEM((n_band, size, PW), BF16),
                pltpu.VMEM((n_band, size, PW), BF16),
                pltpu.VMEM((SPREAD, block, PW), F32),
                pltpu.VMEM((sides, block, PW), F32),
                pltpu.VMEM((block, PW), F32),
                pltpu.VMEM((n_band - 1, block, PW), F32),
                pltpu.SemaphoreType.DMA((n_band, sides)),
                pltpu.SemaphoreType.DMA((n_band, sides)),
                pltpu.SemaphoreType.DMA((n_band,)),
                pltpu.SemaphoreType.DMA((n_band,)),
                pltpu.SemaphoreType.DMA((sides,)),
                pltpu.SemaphoreType.DMA((sides,)),
                pltpu.SemaphoreType.DMA((n_band - 1,)),
                pltpu.SemaphoreType.DMA((n_band - 1,)),
            ],
            compiler_params=pltpu.CompilerParams(
                collective_id=0, has_side_effects=True, vmem_limit_bytes=VMEM_LIMIT
            ),
        )(*arrays)

    return jax.shard_map(
        local,
        mesh=mesh,
        in_specs=(
            P(("ra", "band"), None, None),
            P(("ra", "band")),
            P(("ra", "band")),
            P(("ra", "band")),
            P(("ra", "band")),
            P(("ra", "band")),
            P(),
            P(),
            P(),
            P(),
        ),
        out_specs=(P(None, "band", "ra"), P("band", "ra")),
        check_vma=False,
    )
```
